32 devices in a mesh: song: 2 (over y), seq: 16 (over z, x, core).
Axes of the slice: x: 2, y: 2, z: 4, core: 2. Of those that a mesh axis runs over, the one named last changes fastest.
Arguments:
- song_ids: int32 [4096], P(('song', 'seq')), parts along dimension 0, may hold values from 0 to 2047
- table: bfloat16 [2048, 2432], P(None, 'seq'), may hold values from -6 to 6
- position_table: bfloat16 [2048, 2432], P('seq'), may hold values from -4 to 4
- w_qkv: bfloat16 [2, 2432, 1800], replicated, may hold values from -4 to 4
- w_out: bfloat16 [2, 600, 2432], replicated, may hold values from -0.25 to 0.25
Outputs:
- stream_out: bfloat16 [4096, 2432], P(('song', 'seq')), parts along dimension 0
The draws below stay inside these ranges and needn't reach their ends.
There are 2 independent parts, one for each index of `song`. The reference program is written for one: setup_inputs(seed, part) draws one part's arguments, and reference() takes and returns one part's arrays. A program takes and returns all parts, laid end to end along the dimension named above; an argument that names none is the same for every part. Nothing has to cross between parts.
All inputs are finite; a program needn't handle non-finite values.
Results may differ from the reference program's by a relative error of at most 0.0065.
Values may be sent and summed in bfloat16 or wider, within the bound.
A program may use at most 192 MiB of HBM per device.

```python
import math
import jax
import jax.numpy as jnp
import numpy as np
from jax import lax

D = 2432
HEADS = 4
HEAD = 150
VOCAB = 2048
ROW_TOKENS = 128
LAYERS = 2
ATT = 600
ROWS = 16
TOKENS = 2048


def draw_w_qkv(key, part):
    spread = D ** (-0.5)
    base = jax.random.normal(key, (LAYERS, D, 3 * ATT), jnp.float32) * spread
    base = jnp.clip(base, -6.0 * spread, 6.0 * spread)
    return jnp.clip(base, -4.0, 4.0).astype(jnp.bfloat16)


def plant(drawn, key, low, top_value):
    longest = drawn.shape.index(max(drawn.shape))
    spots = []
    for shift in (0, 1):
        where = [jax.random.randint(jax.random.fold_in(key, axis), (), 0, length) for axis, length in enumerate(drawn.shape)]
        where[longest] = (where[longest] + shift) % drawn.shape[longest]
        spots.append(tuple(where))
    return drawn.at[spots[0]].set(low).at[spots[1]].set(top_value)


def shard_levels(own_key, extent, shards, smallest, top_value):
    gain, own = 1.0, jax.random.fold_in(own_key, 6)
    for position, parts in shards:
        steps = jnp.exp(jax.random.uniform(jax.random.fold_in(own, position), (parts,), jnp.float32, smallest / len(shards), top_value / len(shards)))
        gain = gain * jnp.repeat(steps, extent[position] // parts).reshape([-1 if axis == position else 1 for axis in range(len(extent))])
    return gain


def rank_bounds(amount, slope):
    weights = [(1 << 20) // math.isqrt(rank ** slope) + 1 for rank in range(1, amount + 1)]
    scale = 1 + sum(weights) // (1 << 30)
    return np.cumsum(np.array([max(1, weight // scale) for weight in weights]))


def ranked_ids(key, dims, number_of, skew):
    table = rank_bounds(number_of, skew)
    pick = jax.random.randint(jax.random.fold_in(key, 1), dims, 0, int(table[number_of - 1]))
    standing = jnp.searchsorted(jnp.asarray(table, jnp.int32), pick, side="right")
    return jax.random.permutation(jax.random.fold_in(key, 2), number_of)[standing].astype(jnp.int32)


def noise(rng, dims, width, most, cuts=(), held_as=jnp.bfloat16):
    values = jax.random.normal(rng, dims, jnp.float32) * width
    if len(cuts) > 0:
        values = shard_levels(rng, dims, cuts, -0.22, 0.18) * values
    return jnp.clip(values, min=-most, max=most).astype(held_as)


def setup_inputs(seed: int = 0, part: int = 0) -> dict:
    seeds = jax.random.split(jax.random.key(seed), 6)
    part_keys = jax.random.split(jax.random.fold_in(seeds[5], part), 6)
    song_ids = plant(ranked_ids(part_keys[0], (TOKENS,), VOCAB, 2), jax.random.fold_in(part_keys[0], 3), 0, VOCAB - 1).astype(jnp.int32)
    table = noise(seeds[1], (VOCAB, D), 1.0, 6.0, ((1, 16),))
    position_table = noise(seeds[2], (TOKENS, D), 0.5, 4.0, ((0, 16),))
    w_qkv = draw_w_qkv(jax.random.fold_in(seeds[5], 71), part)
    w_out = noise(seeds[4], (LAYERS, ATT, D), ATT ** -0.5, 0.25)
    return {"song_ids": song_ids, "table": table, "position_table": position_table, "w_qkv": w_qkv, "w_out": w_out}


epsilon = 1e-05

def normalize(residual):
    center_mean = lax.optimization_barrier(jnp.mean(residual, axis=-1, keepdims=True))
    centered = residual - center_mean
    variance = lax.optimization_barrier(jnp.mean(centered * centered, axis=-1, keepdims=True))
    return (centered * lax.rsqrt(variance + epsilon)).astype(jnp.bfloat16)

def project(residual, weight):
    joined = jnp.dot(normalize(residual), weight, preferred_element_type=jnp.float32).astype(jnp.bfloat16)
    return joined.reshape(ROWS, ROW_TOKENS, HEADS, 3 * HEAD).astype(jnp.float32)

def reference(song_ids, table, position_table, w_qkv, w_out):
    inv_root = 1.0 / math.sqrt(HEAD)
    residual = table[song_ids].astype(jnp.float32) + position_table.astype(jnp.float32)
    row_ids = jnp.arange(ROWS)
    joined = project(residual, w_qkv[0])
    query = joined[..., :HEAD]
    keys_col = joined[..., HEAD:2 * HEAD]
    values_col = joined[..., 2 * HEAD:]
    scores = jnp.einsum('rchd,schd->chrs', query, keys_col) * inv_root
    allowed = row_ids[None, :] <= row_ids[:, None]
    scores = jnp.where(allowed, scores, -jnp.inf)
    top_score = lax.optimization_barrier(jnp.max(scores, axis=-1, keepdims=True))
    lifted = jnp.exp(scores - top_score)
    probs = (lifted / lax.optimization_barrier(jnp.sum(lifted, axis=-1, keepdims=True))).astype(jnp.bfloat16).astype(jnp.float32)
    mixed = jnp.einsum('chrs,schd->rchd', probs, values_col).astype(jnp.bfloat16).reshape(TOKENS, ATT)
    residual = residual + jnp.dot(mixed, w_out[0], preferred_element_type=jnp.float32)
    joined = project(residual, w_qkv[1])
    query = joined[..., :HEAD]
    keys_row = joined[..., HEAD:2 * HEAD]
    values_row = joined[..., 2 * HEAD:]
    keys_prev = jnp.concatenate([jnp.zeros_like(keys_row[:1]), keys_row[:-1]], axis=0)
    values_prev = jnp.concatenate([jnp.zeros_like(values_row[:1]), values_row[:-1]], axis=0)
    far_scores = jnp.einsum('rchd,rkhd->rhck', query, keys_prev) * inv_root
    far_scores = jnp.where((row_ids > 0)[:, None, None, None], far_scores, -jnp.inf)
    own_scores = jnp.einsum('rchd,rchd->rhc', query, keys_row)[..., None] * inv_root
    scores = jnp.concatenate([far_scores, own_scores], axis=-1)
    top_score = lax.optimization_barrier(jnp.max(scores, axis=-1, keepdims=True))
    lifted = jnp.exp(scores - top_score)
    probs = (lifted / lax.optimization_barrier(jnp.sum(lifted, axis=-1, keepdims=True))).astype(jnp.bfloat16).astype(jnp.float32)
    far_part = jnp.einsum('rhck,rkhd->rchd', probs[..., :-1], values_prev)
    own_part = jnp.transpose(probs[..., -1], (0, 2, 1))[..., None] * values_row
    mixed = (far_part + own_part).astype(jnp.bfloat16).reshape(TOKENS, ATT)
    residual = residual + jnp.dot(mixed, w_out[1], preferred_element_type=jnp.float32)
    return residual.astype(jnp.bfloat16)
```

```python
import functools
import math

import jax
import jax.numpy as jnp
from jax import lax
from jax.experimental import pallas as pl
from jax.experimental.pallas import tpu as pltpu
from jax.sharding import PartitionSpec as P

HEADS = 4
HEAD = 150
MESH = pl.DeviceIdType.MESH

epsilon = 1e-05
inv_root = 1.0 / math.sqrt(HEAD)


def cuts(width, step):
    return [(a, min(a + step, width)) for a in range(0, width, step)]


def spans(edges):
    return list(zip(edges[:-1], edges[1:]))


def qkv_spans(width):
    return spans([0] + [min(-(-3 * HEAD * (h + 1) // 128) * 128, width) for h in range(HEADS)])


def mix_spans(att):
    edges = [0, 2 * HEAD // 128 * 128, 3 * HEAD // 128 * 128, att]
    return spans(edges)


def normalize_into(resid, normed):
    value = resid[...]
    mean = jnp.mean(value, axis=-1, keepdims=True)
    centered = value - mean
    variance = jnp.mean(centered * centered, axis=-1, keepdims=True)
    normed[...] = (centered * lax.rsqrt(variance + epsilon)).astype(jnp.bfloat16)


def dot_nt(a, b):
    dims = (((1,), (1,)), ((), ()))
    return lax.dot_general(a, b, dims, preferred_element_type=jnp.float32)


def scores_of(q, k):
    return dot_nt(q, k) * inv_root


def kernel(n, ids_hbm, table_hbm, pos_hbm, wqkv_hbm, wout_hbm, out_ref,
           pos_v, wq_v, wo_v, table_t, ids_all, emb_s, emb_r, emb_t, resid, normed,
           qkv_s, qkv_r, wide, mix_s, mix_r, mixed, kv_s, kv_r,
           load_sem, ids_ss, ids_rs, emb_ss, emb_rs, qkv_ss, qkv_rs, mix_ss, mix_rs, kv_ss, kv_rs):
    me = lax.axis_index("seq")
    features, vocab = table_t.shape
    tokens, depth = resid.shape
    cols = tokens // n
    width = wide.shape[1]
    att = mixed.shape[1]
    others = list(range(n // 2, n)) + list(range(1, n // 2))

    def send(src, dst, ss, rs, k):
        return pltpu.make_async_remote_copy(
            src_ref=src, dst_ref=dst, send_sem=ss, recv_sem=rs,
            device_id={"seq": me ^ k}, device_id_type=MESH)

    def settle(ref, sem):
        pltpu.make_async_copy(ref, ref, sem).wait()

    def settle_all(ref, sem):
        settle(ref.at[pl.ds(0, n - 1)], sem)

    loads = [pltpu.make_async_copy(table_hbm, table_t, load_sem.at[0]),
             pltpu.make_async_copy(pos_hbm, pos_v, load_sem.at[1])]
    for layer in range(2):
        loads.append(pltpu.make_async_copy(wqkv_hbm.at[layer], wq_v.at[layer], load_sem.at[2 + 2 * layer]))
        loads.append(pltpu.make_async_copy(wout_hbm.at[layer], wo_v.at[layer], load_sem.at[3 + 2 * layer]))
    own_ids = ids_all.at[me]
    ids_load = pltpu.make_async_copy(ids_hbm, own_ids, load_sem.at[6])
    ids_load.start()
    loads[0].start()

    barrier = pltpu.get_barrier_semaphore()
    for k in others:
        pl.semaphore_signal(barrier, inc=1, device_id={"seq": me ^ k}, device_id_type=MESH)
    ids_load.wait()
    pl.semaphore_wait(barrier, n - 1)

    for k in others:
        send(own_ids, own_ids, ids_ss, ids_rs.at[k], k).start()
    loads[0].wait()
    for load in loads[1:]:
        load.start()

    def gather(ids):
        codes = lax.broadcasted_iota(jnp.int32, (vocab, tokens), 0)
        hot = jnp.where(codes == ids, 1.0, 0.0).astype(jnp.bfloat16)
        return jnp.dot(table_t[...], hot, preferred_element_type=jnp.float32).astype(jnp.bfloat16)

    def serve(step, carry):
        k = 1 + lax.rem(n // 2 - 1 + step, n - 1)
        peer = me ^ k
        settle(ids_all.at[peer], ids_rs.at[k])
        emb_s[peer] = gather(ids_all[peer])
        send(emb_s.at[peer], emb_r.at[me], emb_ss, emb_rs, k).start()
        return carry

    lax.fori_loop(0, n - 1, serve, 0)
    emb_r[me] = gather(ids_all[me])
    settle_all(emb_r, emb_rs)
    for src in range(n):
        emb_t[src * features:(src + 1) * features, :] = emb_r[src].astype(jnp.float32)
    loads[1].wait()
    for a, b in cuts(depth, 128):
        resid[:, a:b] = emb_t[a:b, :].T + pos_v[:, a:b].astype(jnp.float32)

    normalize_into(resid, normed)
    loads[2].wait()
    qkv = qkv_spans(width)
    for part, (a, b) in enumerate(qkv):
        wide[:, a:b] = dot_nt(normed[...], wq_v[0, a:b, :])
        for dst in range(n):
            qkv_s[part][dst] = wide[dst * cols:(dst + 1) * cols, a:b].astype(jnp.bfloat16)
        for k in others:
            send(qkv_s[part].at[me ^ k], qkv_r[part].at[me], qkv_ss.at[part], qkv_rs.at[part], k).start()
        qkv_r[part][me] = qkv_s[part][me]

    first = lax.broadcasted_iota(jnp.int32, (tokens, tokens), 0)
    second = lax.broadcasted_iota(jnp.int32, (tokens, tokens), 1)
    allowed = (((first - second) & (cols - 1)) == 0) & (second <= first)
    mix = mix_spans(att)
    sent = 0
    for h in range(HEADS):
        a, b = qkv[h]
        settle_all(qkv_r[h], qkv_rs.at[h])
        for src in range(n):
            wide[src * cols:(src + 1) * cols, a:b] = qkv_r[h][src].astype(jnp.float32)
        at = 3 * HEAD * h
        q = wide[:, at:at + HEAD].astype(jnp.bfloat16)
        k = wide[:, at + HEAD:at + 2 * HEAD].astype(jnp.bfloat16)
        v = wide[:, at + 2 * HEAD:at + 3 * HEAD].astype(jnp.bfloat16)
        scores = jnp.where(allowed, scores_of(q, k), -jnp.inf)
        lifted = jnp.exp(scores - jnp.max(scores, axis=-1, keepdims=True))
        probs = (lifted / jnp.sum(lifted, axis=-1, keepdims=True)).astype(jnp.bfloat16)
        mixed[:, HEAD * h:HEAD * (h + 1)] = jnp.dot(probs, v, preferred_element_type=jnp.float32)
        while sent < len(mix) and mix[sent][1] <= HEAD * (h + 1):
            a, b = mix[sent]
            for dst in range(n):
                mix_s[sent][dst] = mixed[dst * cols:(dst + 1) * cols, a:b].astype(jnp.bfloat16)
            for k in others:
                send(mix_s[sent].at[me ^ k], mix_r[sent].at[me], mix_ss.at[sent], mix_rs.at[sent], k).start()
            mix_r[sent][me] = mix_s[sent][me]
            sent += 1

    def receive_mix(part):
        a, b = mix[part]
        settle_all(mix_r[part], mix_rs.at[part])
        for src in range(n):
            mixed[src * cols:(src + 1) * cols, a:b] = mix_r[part][src].astype(jnp.float32)

    loads[3].wait()
    for parts in ((0,), tuple(range(1, len(mix)))):
        for part in parts:
            receive_mix(part)
        lo, hi = mix[parts[0]][0], mix[parts[-1]][1]
        back = mixed[:, lo:hi].astype(jnp.bfloat16)
        for a, b in cuts(depth, 512):
            resid[:, a:b] += jnp.dot(back, wo_v[0, lo:hi, a:b], preferred_element_type=jnp.float32)
    normalize_into(resid, normed)
    loads[4].wait()

    def shift(part):
        return pltpu.make_async_remote_copy(
            src_ref=kv_s[part], dst_ref=kv_r[part], send_sem=kv_ss.at[part], recv_sem=kv_rs.at[part],
            device_id={"seq": lax.rem(me + 1, n)}, device_id_type=MESH)

    @pl.when(me == 0)
    def _():
        for part in range(HEADS):
            kv_r[part][...] = jnp.zeros_like(kv_r[part])

    for part, (a, b) in enumerate(qkv):
        wide[:, a:b] = dot_nt(normed[...], wq_v[1, a:b, :])
        at = 3 * HEAD * part + HEAD
        kv_s[part][...] = wide[:, at:at + 2 * HEAD].astype(jnp.bfloat16)

        @pl.when(me < n - 1)
        def _():
            shift(part).start()

    owns = []
    for h in range(HEADS):
        at = 3 * HEAD * h
        q = wide[:, at:at + HEAD].astype(jnp.bfloat16)
        k_own = wide[:, at + HEAD:at + 2 * HEAD].astype(jnp.bfloat16).astype(jnp.float32)
        own = jnp.sum(q.astype(jnp.float32) * k_own, axis=-1, keepdims=True) * inv_root
        owns.append(own)

    loads[5].wait()
    for h in range(HEADS):
        @pl.when(me > 0)
        def _():
            shift(h).wait_recv()
        at = 3 * HEAD * h
        q = wide[:, at:at + HEAD].astype(jnp.bfloat16)
        v_own = wide[:, at + 2 * HEAD:at + 3 * HEAD].astype(jnp.bfloat16).astype(jnp.float32)
        k = kv_r[h][:, :HEAD]
        v = kv_r[h][:, HEAD:]
        own = owns[h]
        far = jnp.where(me > 0, scores_of(q, k), -jnp.inf)
        top = jnp.maximum(jnp.max(far, axis=-1, keepdims=True), own)
        far_lifted = jnp.exp(far - top)
        own_lifted = jnp.exp(own - top)
        total = jnp.sum(far_lifted, axis=-1, keepdims=True) + own_lifted
        far_probs = (far_lifted / total).astype(jnp.bfloat16)
        own_probs = (own_lifted / total).astype(jnp.bfloat16).astype(jnp.float32)
        mixed[:, HEAD * h:HEAD * (h + 1)] = (
            jnp.dot(far_probs, v, preferred_element_type=jnp.float32) + own_probs * v_own)
        if h == 1:
            lo, hi = mix[0]
            back = mixed[:, lo:hi].astype(jnp.bfloat16)
            for a, b in cuts(depth, 512):
                resid[:, a:b] += jnp.dot(back, wo_v[1, lo:hi, a:b], preferred_element_type=jnp.float32)

    lo, hi = mix[1][0], mix[-1][1]
    back = mixed[:, lo:hi].astype(jnp.bfloat16)
    for a, b in cuts(depth, 512):
        out_ref[:, a:b] = (resid[:, a:b] + jnp.dot(
            back, wo_v[1, lo:hi, a:b], preferred_element_type=jnp.float32)).astype(jnp.bfloat16)

    settle_all(ids_all, ids_ss)
    settle_all(emb_s, emb_ss)
    for part in range(HEADS):
        settle_all(qkv_s[part], qkv_ss.at[part])
    for part in range(len(mix)):
        settle_all(mix_s[part], mix_ss.at[part])

    @pl.when(me < n - 1)
    def _():
        for part in range(HEADS):
            shift(part).wait_send()


def solution(mesh):
    n = mesh.shape["seq"]

    def shards(song_ids, table, position_table, w_qkv, w_out):
        tokens, depth = position_table.shape
        vocab, features = table.shape
        layers, _, width = w_qkv.shape
        att = w_out.shape[1]
        cols = tokens // n
        bf16, f32 = jnp.bfloat16, jnp.float32
        hbm = pl.BlockSpec(memory_space=pl.ANY)
        qkv = [pltpu.VMEM((n, cols, b - a), bf16) for a, b in qkv_spans(width)]
        mix = [pltpu.VMEM((n, cols, b - a), bf16) for a, b in mix_spans(att)]
        kv = [pltpu.VMEM((tokens, 2 * HEAD), bf16)] * HEADS
        sems = pltpu.SemaphoreType.DMA
        return pl.pallas_call(
            functools.partial(kernel, n),
            out_shape=pltpu.VMEM((tokens, depth), bf16),
            in_specs=[hbm, hbm, hbm, hbm, hbm],
            out_specs=pl.BlockSpec(memory_space=pltpu.VMEM),
            scratch_shapes=[
                pltpu.VMEM((tokens, depth), bf16),
                pltpu.VMEM((layers, width, depth), bf16),
                pltpu.VMEM((layers, att, depth), bf16),
                pltpu.VMEM((features, vocab), bf16),
                pltpu.VMEM((n, 1, tokens), jnp.int32),
                pltpu.VMEM((n, features, tokens), bf16),
                pltpu.VMEM((n, features, tokens), bf16),
                pltpu.VMEM((depth, tokens), f32),
                pltpu.VMEM((tokens, depth), f32),
                pltpu.VMEM((tokens, depth), bf16),
                qkv, list(qkv),
                pltpu.VMEM((tokens, width), f32),
                mix, list(mix),
                pltpu.VMEM((tokens, att), f32),
                kv, list(kv),
                sems((7,)),
                sems, sems((n,)), sems, sems,
                sems((HEADS,)), sems((HEADS,)), sems((len(mix),)), sems((len(mix),)),
                sems((HEADS,)), sems((HEADS,)),
            ],
            compiler_params=pltpu.CompilerParams(
                collective_id=0, has_side_effects=True, vmem_limit_bytes=56 << 20),
            name="music_rows",
        )(song_ids.reshape(1, tokens), table.T, position_table, jnp.swapaxes(w_qkv, 1, 2), w_out)

    in_specs = (P(("song", "seq")), P(None, "seq"), P("seq", None), P(), P())
    out_specs = P(("song", "seq"), None)
    return jax.shard_map(shards, mesh=mesh, in_specs=in_specs, out_specs=out_specs, check_vma=False)
```

```python
import functools
import math

import jax
import jax.numpy as jnp
from jax import lax
from jax.experimental import pallas as pl
from jax.experimental.pallas import tpu as pltpu
from jax.sharding import PartitionSpec as P

HEADS = 4
HEAD = 150
MESH = pl.DeviceIdType.MESH

epsilon = 1e-05
inv_root = 1.0 / math.sqrt(HEAD)


def cuts(width, step):
    return [(a, min(a + step, width)) for a in range(0, width, step)]


def spans(edges):
    return list(zip(edges[:-1], edges[1:]))


def head_spans(width):
    return spans([0] + [min(-(-3 * HEAD * (h + 1) // 128) * 128, width) for h in range(HEADS)])


def qkv_spans(width):
    heads = head_spans(width)
    return [(heads[h][0], heads[h + 1][1]) for h in range(0, HEADS, 2)]


def mix_spans(att):
    return spans([0, 2 * HEAD // 128 * 128, att])


def normalize_into(resid, normed):
    value = resid[...]
    mean = jnp.mean(value, axis=-1, keepdims=True)
    centered = value - mean
    variance = jnp.mean(centered * centered, axis=-1, keepdims=True)
    normed[...] = (centered * lax.rsqrt(variance + epsilon)).astype(jnp.bfloat16)


def dot_nt(a, b):
    dims = (((1,), (1,)), ((), ()))
    return lax.dot_general(a, b, dims, preferred_element_type=jnp.float32)


def scores_of(q, k):
    return dot_nt(q, k) * inv_root


def kernel(n, ids_hbm, table_hbm, pos_hbm, wqkv_hbm, wout_hbm, out_ref,
           pos_v, wq_v, wo_v, table_t, ids_all, emb_s, emb_r, emb_t, resid, normed,
           qkv_s, qkv_r, wt, wide, mix_s, mix_r, mixed, kv_s, kv_r,
           load_sem, ids_ss, ids_rs, emb_ss, emb_rs, qkv_ss, qkv_rs, mix_ss, mix_rs, kv_ss, kv_rs):
    me = lax.axis_index("seq")
    features, vocab = table_t.shape
    tokens, depth = resid.shape
    cols = tokens // n
    width = wide.shape[1]
    att = mixed.shape[1]
    others = list(range(n // 2, n)) + list(range(1, n // 2))
    parity = me & 1

    def send(src, dst, ss, rs, k):
        return pltpu.make_async_remote_copy(
            src_ref=src, dst_ref=dst, send_sem=ss, recv_sem=rs,
            device_id={"seq": me ^ k}, device_id_type=MESH)

    def settle(ref, sem):
        pltpu.make_async_copy(ref, ref, sem).wait()

    def settle_all(ref, sem):
        settle(ref.at[pl.ds(0, n - 1)], sem)

    loads = [pltpu.make_async_copy(table_hbm, table_t, load_sem.at[0]),
             pltpu.make_async_copy(pos_hbm, pos_v, load_sem.at[1])]
    for layer in range(2):
        loads.append(pltpu.make_async_copy(wqkv_hbm.at[layer], wq_v.at[layer], load_sem.at[2 + 2 * layer]))
        loads.append(pltpu.make_async_copy(wout_hbm.at[layer], wo_v.at[layer], load_sem.at[3 + 2 * layer]))
    own_ids = ids_all.at[me]
    ids_load = pltpu.make_async_copy(ids_hbm, own_ids, load_sem.at[6])
    ids_load.start()
    loads[0].start()

    barrier = pltpu.get_barrier_semaphore()
    for k in others:
        pl.semaphore_signal(barrier, inc=1, device_id={"seq": me ^ k}, device_id_type=MESH)
    ids_load.wait()
    pl.semaphore_wait(barrier, n - 1)

    for k in others:
        send(own_ids, own_ids, ids_ss, ids_rs.at[k], k).start()
    loads[0].wait()
    for load in loads[1:]:
        load.start()

    def gather(ids):
        codes = lax.broadcasted_iota(jnp.int32, (vocab, tokens), 0)
        hot = jnp.where(codes == ids, 1.0, 0.0).astype(jnp.bfloat16)
        return jnp.dot(table_t[...], hot, preferred_element_type=jnp.float32).astype(jnp.bfloat16)

    def serve(step, carry):
        group, turn = step // (n // 2), lax.rem(step, n // 2)
        k = 2 * lax.rem(turn + n // 4, n // 2) + (group ^ parity)
        peer = me ^ k

        @pl.when(k > 0)
        def _():
            settle(ids_all.at[peer], ids_rs.at[k])

        emb_s[peer] = gather(ids_all[peer])

        @pl.when(k > 0)
        def _():
            send(emb_s.at[peer], emb_r.at[me], emb_ss, emb_rs, k).start()
        return carry

    lax.fori_loop(0, n, serve, 0)
    emb_r[me] = emb_s[me]

    def turn_weights():
        loads[4].wait()

        def strip(i, carry):
            at = pl.multiple_of(i * 128, 128)
            for a, b in cuts(width, 128):
                wt[pl.ds(at, 128), a:b] = wq_v[1, a:b, pl.ds(at, 128)].T
            return carry

        lax.fori_loop(0, depth // 128, strip, 0)

    @pl.when(parity == 1)
    def _():
        turn_weights()

    settle_all(emb_r, emb_rs)
    for src in range(n):
        emb_t[src * features:(src + 1) * features, :] = emb_r[src].astype(jnp.float32)
    loads[1].wait()
    for a, b in cuts(depth, 128):
        resid[:, a:b] = emb_t[a:b, :].T + pos_v[:, a:b].astype(jnp.float32)

    normalize_into(resid, normed)
    loads[2].wait()
    qkv = qkv_spans(width)
    for part, (a, b) in enumerate(qkv):
        wide[:, a:b] = dot_nt(normed[...], wq_v[0, a:b, :])
        for dst in range(n):
            qkv_s[part][dst] = wide[dst * cols:(dst + 1) * cols, a:b].astype(jnp.bfloat16)
        for k in others:
            send(qkv_s[part].at[me ^ k], qkv_r[part].at[me], qkv_ss.at[part], qkv_rs.at[part], k).start()
        qkv_r[part][me] = qkv_s[part][me]

    @pl.when(parity == 0)
    def _():
        turn_weights()

    first = lax.broadcasted_iota(jnp.int32, (tokens, tokens), 0)
    second = lax.broadcasted_iota(jnp.int32, (tokens, tokens), 1)
    allowed = (((first - second) & (cols - 1)) == 0) & (second <= first)
    mix = mix_spans(att)
    sent = 0
    for h in range(HEADS):
        if h % 2 == 0:
            part = h // 2
            a, b = qkv[part]
            settle_all(qkv_r[part], qkv_rs.at[part])
            for src in range(n):
                wide[src * cols:(src + 1) * cols, a:b] = qkv_r[part][src].astype(jnp.float32)
        at = 3 * HEAD * h
        q = wide[:, at:at + HEAD].astype(jnp.bfloat16)
        k = wide[:, at + HEAD:at + 2 * HEAD].astype(jnp.bfloat16)
        v = wide[:, at + 2 * HEAD:at + 3 * HEAD].astype(jnp.bfloat16)
        scores = jnp.where(allowed, scores_of(q, k), -jnp.inf)
        lifted = jnp.exp(scores - jnp.max(scores, axis=-1, keepdims=True))
        probs = (lifted / jnp.sum(lifted, axis=-1, keepdims=True)).astype(jnp.bfloat16)
        mixed[:, HEAD * h:HEAD * (h + 1)] = jnp.dot(probs, v, preferred_element_type=jnp.float32)
        while sent < len(mix) and mix[sent][1] <= HEAD * (h + 1):
            a, b = mix[sent]
            for dst in range(n):
                mix_s[sent][dst] = mixed[dst * cols:(dst + 1) * cols, a:b].astype(jnp.bfloat16)
            for k in others:
                send(mix_s[sent].at[me ^ k], mix_r[sent].at[me], mix_ss.at[sent], mix_rs.at[sent], k).start()
            mix_r[sent][me] = mix_s[sent][me]
            sent += 1

    def receive_mix(part):
        a, b = mix[part]
        settle_all(mix_r[part], mix_rs.at[part])
        for src in range(n):
            mixed[src * cols:(src + 1) * cols, a:b] = mix_r[part][src].astype(jnp.float32)

    loads[3].wait()
    for parts in ((0,), tuple(range(1, len(mix)))):
        for part in parts:
            receive_mix(part)
        lo, hi = mix[parts[0]][0], mix[parts[-1]][1]
        back = mixed[:, lo:hi].astype(jnp.bfloat16)
        for a, b in cuts(depth, 512):
            resid[:, a:b] += jnp.dot(back, wo_v[0, lo:hi, a:b], preferred_element_type=jnp.float32)
    normalize_into(resid, normed)

    def shift(part):
        return pltpu.make_async_remote_copy(
            src_ref=kv_s[part], dst_ref=kv_r[part], send_sem=kv_ss.at[part], recv_sem=kv_rs.at[part],
            device_id={"seq": lax.rem(me + 1, n)}, device_id_type=MESH)

    @pl.when(me == 0)
    def _():
        for part in range(HEADS):
            kv_r[part][...] = jnp.zeros_like(kv_r[part])

    for part, (a, b) in enumerate(head_spans(width)):
        wide[:, a:b] = jnp.dot(normed[...], wt[:, a:b], preferred_element_type=jnp.float32)
        at = 3 * HEAD * part + HEAD
        kv_s[part][...] = wide[:, at:at + 2 * HEAD].astype(jnp.bfloat16)

        @pl.when(me < n - 1)
        def _():
            shift(part).start()

    owns = []
    for h in range(HEADS):
        at = 3 * HEAD * h
        q = wide[:, at:at + HEAD].astype(jnp.bfloat16)
        k_own = wide[:, at + HEAD:at + 2 * HEAD].astype(jnp.bfloat16).astype(jnp.float32)
        own = jnp.sum(q.astype(jnp.float32) * k_own, axis=-1, keepdims=True) * inv_root
        owns.append(own)

    loads[5].wait()
    for h in range(HEADS):
        @pl.when(me > 0)
        def _():
            shift(h).wait_recv()
        at = 3 * HEAD * h
        q = wide[:, at:at + HEAD].astype(jnp.bfloat16)
        v_own = wide[:, at + 2 * HEAD:at + 3 * HEAD].astype(jnp.bfloat16).astype(jnp.float32)
        k = kv_r[h][:, :HEAD]
        v = kv_r[h][:, HEAD:]
        own = owns[h]
        far = jnp.where(me > 0, scores_of(q, k), -jnp.inf)
        top = jnp.maximum(jnp.max(far, axis=-1, keepdims=True), own)
        far_lifted = jnp.exp(far - top)
        own_lifted = jnp.exp(own - top)
        total = jnp.sum(far_lifted, axis=-1, keepdims=True) + own_lifted
        far_probs = (far_lifted / total).astype(jnp.bfloat16)
        own_probs = (own_lifted / total).astype(jnp.bfloat16).astype(jnp.float32)
        mixed[:, HEAD * h:HEAD * (h + 1)] = (
            jnp.dot(far_probs, v, preferred_element_type=jnp.float32) + own_probs * v_own)
        if h == 1:
            lo, hi = mix[0]
            back = mixed[:, lo:hi].astype(jnp.bfloat16)
            for a, b in cuts(depth, 512):
                resid[:, a:b] += jnp.dot(back, wo_v[1, lo:hi, a:b], preferred_element_type=jnp.float32)

    lo, hi = mix[1][0], mix[-1][1]
    back = mixed[:, lo:hi].astype(jnp.bfloat16)
    for a, b in cuts(depth, 512):
        out_ref[:, a:b] = (resid[:, a:b] + jnp.dot(
            back, wo_v[1, lo:hi, a:b], preferred_element_type=jnp.float32)).astype(jnp.bfloat16)

    settle_all(ids_all, ids_ss)
    settle_all(emb_s, emb_ss)
    for part in range(len(qkv)):
        settle_all(qkv_s[part], qkv_ss.at[part])
    for part in range(len(mix)):
        settle_all(mix_s[part], mix_ss.at[part])

    @pl.when(me < n - 1)
    def _():
        for part in range(HEADS):
            shift(part).wait_send()


def solution(mesh):
    n = mesh.shape["seq"]

    def shards(song_ids, table, position_table, w_qkv, w_out):
        tokens, depth = position_table.shape
        vocab, features = table.shape
        layers, _, width = w_qkv.shape
        att = w_out.shape[1]
        cols = tokens // n
        bf16, f32 = jnp.bfloat16, jnp.float32
        hbm = pl.BlockSpec(memory_space=pl.ANY)
        qkv = [pltpu.VMEM((n, cols, b - a), bf16) for a, b in qkv_spans(width)]
        mix = [pltpu.VMEM((n, cols, b - a), bf16) for a, b in mix_spans(att)]
        kv = [pltpu.VMEM((tokens, 2 * HEAD), bf16)] * HEADS
        sems = pltpu.SemaphoreType.DMA
        return pl.pallas_call(
            functools.partial(kernel, n),
            out_shape=pltpu.VMEM((tokens, depth), bf16),
            in_specs=[hbm, hbm, hbm, hbm, hbm],
            out_specs=pl.BlockSpec(memory_space=pltpu.VMEM),
            scratch_shapes=[
                pltpu.VMEM((tokens, depth), bf16),
                pltpu.VMEM((layers, width, depth), bf16),
                pltpu.VMEM((layers, att, depth), bf16),
                pltpu.VMEM((features, vocab), bf16),
                pltpu.VMEM((n, 1, tokens), jnp.int32),
                pltpu.VMEM((n, features, tokens), bf16),
                pltpu.VMEM((n, features, tokens), bf16),
                pltpu.VMEM((depth, tokens), f32),
                pltpu.VMEM((tokens, depth), f32),
                pltpu.VMEM((tokens, depth), bf16),
                qkv, list(qkv),
                pltpu.VMEM((depth, width), bf16),
                pltpu.VMEM((tokens, width), f32),
                mix, list(mix),
                pltpu.VMEM((tokens, att), f32),
                kv, list(kv),
                sems((7,)),
                sems, sems((n,)), sems, sems,
                sems((len(qkv),)), sems((len(qkv),)), sems((len(mix),)), sems((len(mix),)),
                sems((HEADS,)), sems((HEADS,)),
            ],
            compiler_params=pltpu.CompilerParams(
                collective_id=0, has_side_effects=True, vmem_limit_bytes=56 << 20),
            name="music_rows",
        )(song_ids.reshape(1, tokens), table.T, position_table, jnp.swapaxes(w_qkv, 1, 2), w_out)

    in_specs = (P(("song", "seq")), P(None, "seq"), P("seq", None), P(), P())
    out_specs = P(("song", "seq"), None)
    return jax.shard_map(shards, mesh=mesh, in_specs=in_specs, out_specs=out_specs, check_vma=False)
```

```python
import functools
import math

import jax
import jax.numpy as jnp
from jax import lax
from jax.experimental import pallas as pl
from jax.experimental.pallas import tpu as pltpu
from jax.sharding import PartitionSpec as P

HEADS = 4
HEAD = 150
MESH = pl.DeviceIdType.MESH

epsilon = 1e-05
inv_root = 1.0 / math.sqrt(HEAD)


def cuts(width, step):
    return [(a, min(a + step, width)) for a in range(0, width, step)]


def spans(edges):
    return list(zip(edges[:-1], edges[1:]))


def head_spans(width):
    return spans([0] + [min(-(-3 * HEAD * (h + 1) // 128) * 128, width) for h in range(HEADS)])


def qkv_spans(width):
    heads = head_spans(width)
    return [(heads[h][0], heads[h + 1][1]) for h in range(0, HEADS, 2)]


def mix_spans(att):
    return spans([0, 2 * HEAD // 128 * 128, att])


def normalize_into(resid, normed):
    value = resid[...]
    mean = jnp.mean(value, axis=-1, keepdims=True)
    centered = value - mean
    variance = jnp.mean(centered * centered, axis=-1, keepdims=True)
    normed[...] = (centered * lax.rsqrt(variance + epsilon)).astype(jnp.bfloat16)


def dot_nt(a, b):
    dims = (((1,), (1,)), ((), ()))
    return lax.dot_general(a, b, dims, preferred_element_type=jnp.float32)


def scores_of(q, k):
    return dot_nt(q, k) * inv_root


def kernel(n, ids_hbm, table_hbm, pos_hbm, wqkv_hbm, wout_hbm, out_ref,
           pos_v, wq_v, wo_v, table_t, ids_all, emb_s, emb_r, emb_t, resid, normed,
           qkv_s, qkv_r, wt, wide, mix_s, mix_r, mixed, kv_s, kv_r,
           load_sem, ids_ss, ids_rs, emb_ss, emb_rs, qkv_ss, qkv_rs, mix_ss, mix_rs, kv_ss, kv_rs):
    me = lax.axis_index("seq")
    features, vocab = table_t.shape
    tokens, depth = resid.shape
    cols = tokens // n
    width = wide.shape[1]
    att = mixed.shape[1]
    others = list(range(n // 2, n)) + list(range(1, n // 2))
    parity = me & 1

    def send(src, dst, ss, rs, k):
        return pltpu.make_async_remote_copy(
            src_ref=src, dst_ref=dst, send_sem=ss, recv_sem=rs,
            device_id={"seq": me ^ k}, device_id_type=MESH)

    def settle(ref, sem):
        pltpu.make_async_copy(ref, ref, sem).wait()

    def settle_all(ref, sem):
        settle(ref.at[pl.ds(0, n - 1)], sem)

    loads = [pltpu.make_async_copy(table_hbm, table_t, load_sem.at[0]),
             pltpu.make_async_copy(pos_hbm, pos_v, load_sem.at[1])]
    for layer in range(2):
        loads.append(pltpu.make_async_copy(wqkv_hbm.at[layer], wq_v.at[layer], load_sem.at[2 + 2 * layer]))
        loads.append(pltpu.make_async_copy(wout_hbm.at[layer], wo_v.at[layer], load_sem.at[3 + 2 * layer]))
    own_ids = ids_all.at[me]
    ids_load = pltpu.make_async_copy(ids_hbm, own_ids, load_sem.at[6])
    ids_load.start()
    loads[0].start()

    barrier = pltpu.get_barrier_semaphore()
    for k in others:
        pl.semaphore_signal(barrier, inc=1, device_id={"seq": me ^ k}, device_id_type=MESH)
    ids_load.wait()
    pl.semaphore_wait(barrier, n - 1)

    for k in others:
        send(own_ids, own_ids, ids_ss, ids_rs.at[k], k).start()
    loads[0].wait()
    for load in loads[1:]:
        load.start()

    def gather(ids):
        codes = lax.broadcasted_iota(jnp.int32, (vocab, tokens), 0)
        hot = jnp.where(codes == ids, 1.0, 0.0).astype(jnp.bfloat16)
        return jnp.dot(table_t[...], hot, preferred_element_type=jnp.float32).astype(jnp.bfloat16)

    def serve(step, carry):
        group, turn = step // (n // 2), lax.rem(step, n // 2)
        k = 2 * lax.rem(turn + n // 4, n // 2) + (group ^ parity)
        peer = me ^ k

        @pl.when(k > 0)
        def _():
            settle(ids_all.at[peer], ids_rs.at[k])

        emb_s[peer] = gather(ids_all[peer])

        @pl.when(k > 0)
        def _():
            send(emb_s.at[peer], emb_r.at[me], emb_ss, emb_rs, k).start()
        return carry

    lax.fori_loop(0, n, serve, 0)
    emb_r[me] = emb_s[me]

    def turn_weights():
        loads[4].wait()

        def strip(i, carry):
            at = pl.multiple_of(i * 128, 128)
            for a, b in cuts(width, 128):
                wt[pl.ds(at, 128), a:b] = wq_v[1, a:b, pl.ds(at, 128)].T
            return carry

        lax.fori_loop(0, depth // 128, strip, 0)

    @pl.when(parity == 1)
    def _():
        turn_weights()

    settle_all(emb_r, emb_rs)
    for src in range(n):
        emb_t[src * features:(src + 1) * features, :] = emb_r[src].astype(jnp.float32)
    loads[1].wait()
    for a, b in cuts(depth, 128):
        resid[:, a:b] = emb_t[a:b, :].T + pos_v[:, a:b].astype(jnp.float32)

    normalize_into(resid, normed)
    loads[2].wait()
    qkv = qkv_spans(width)
    for part, (a, b) in enumerate(qkv):
        wide[:, a:b] = dot_nt(normed[...], wq_v[0, a:b, :])
        for dst in range(n):
            qkv_s[part][dst] = wide[dst * cols:(dst + 1) * cols, a:b].astype(jnp.bfloat16)
        for k in others:
            send(qkv_s[part].at[me ^ k], qkv_r[part].at[me], qkv_ss.at[part], qkv_rs.at[part], k).start()
        qkv_r[part][me] = qkv_s[part][me]

    @pl.when(parity == 0)
    def _():
        turn_weights()

    first = lax.broadcasted_iota(jnp.int32, (tokens, tokens), 0)
    second = lax.broadcasted_iota(jnp.int32, (tokens, tokens), 1)
    allowed = (((first - second) & (cols - 1)) == 0) & (second <= first)
    mix = mix_spans(att)
    sent = 0
    for h in range(HEADS):
        if h % 2 == 0:
            part = h // 2
            a, b = qkv[part]
            settle_all(qkv_r[part], qkv_rs.at[part])
            for src in range(n):
                wide[src * cols:(src + 1) * cols, a:b] = qkv_r[part][src].astype(jnp.float32)
        at = 3 * HEAD * h
        q = wide[:, at:at + HEAD].astype(jnp.bfloat16)
        k = wide[:, at + HEAD:at + 2 * HEAD].astype(jnp.bfloat16)
        v = wide[:, at + 2 * HEAD:at + 3 * HEAD].astype(jnp.bfloat16)
        scores = jnp.where(allowed, scores_of(q, k), -jnp.inf)
        lifted = jnp.exp(scores - jnp.max(scores, axis=-1, keepdims=True))
        probs = (lifted / jnp.sum(lifted, axis=-1, keepdims=True)).astype(jnp.bfloat16)
        mixed[:, HEAD * h:HEAD * (h + 1)] = jnp.dot(probs, v, preferred_element_type=jnp.float32)
        while sent < len(mix) and mix[sent][1] <= HEAD * (h + 1):
            a, b = mix[sent]
            for dst in range(n):
                mix_s[sent][dst] = mixed[dst * cols:(dst + 1) * cols, a:b].astype(jnp.bfloat16)
            for k in others:
                send(mix_s[sent].at[me ^ k], mix_r[sent].at[me], mix_ss.at[sent], mix_rs.at[sent], k).start()
            mix_r[sent][me] = mix_s[sent][me]
            sent += 1

    def receive_mix(part):
        a, b = mix[part]
        settle_all(mix_r[part], mix_rs.at[part])
        for src in range(n):
            mixed[src * cols:(src + 1) * cols, a:b] = mix_r[part][src].astype(jnp.float32)

    loads[3].wait()
    for part, (lo, hi) in enumerate(mix):
        receive_mix(part)
        back = mixed[:, lo:hi].astype(jnp.bfloat16)
        shift_by, first_sum, second_sum = None, None, None
        for a, b in cuts(depth, 512):
            value = resid[:, a:b] + jnp.dot(back, wo_v[0, lo:hi, a:b], preferred_element_type=jnp.float32)
            resid[:, a:b] = value
            if part < len(mix) - 1:
                continue
            if shift_by is None:
                shift_by = jnp.mean(value[:, :128], axis=-1, keepdims=True)
                first_sum = jnp.zeros((tokens, 128), jnp.float32)
                second_sum = jnp.zeros((tokens, 128), jnp.float32)
            for c in range(0, b - a, 128):
                off = value[:, c:c + 128] - shift_by
                first_sum += off
                second_sum += off * off
    off_mean = jnp.sum(first_sum, axis=-1, keepdims=True) * (1.0 / depth)
    variance = jnp.sum(second_sum, axis=-1, keepdims=True) * (1.0 / depth) - off_mean * off_mean
    scale = lax.rsqrt(variance + epsilon)
    center = shift_by + off_mean
    for a, b in cuts(depth, 512):
        normed[:, a:b] = ((resid[:, a:b] - center) * scale).astype(jnp.bfloat16)

    def shift(kind, head):
        return pltpu.make_async_remote_copy(
            src_ref=kv_s[kind].at[head], dst_ref=kv_r[kind].at[head],
            send_sem=kv_ss.at[kind, head], recv_sem=kv_rs.at[kind, head],
            device_id={"seq": lax.rem(me + 1, n)}, device_id_type=MESH)

    @pl.when(me == 0)
    def _():
        for kind in range(2):
            kv_r[kind][...] = jnp.zeros_like(kv_r[kind])

    for head, (a, b) in enumerate(head_spans(width)):
        wide[:, a:b] = jnp.dot(normed[...], wt[:, a:b], preferred_element_type=jnp.float32)
        for kind in range(2):
            at = 3 * HEAD * head + HEAD * (kind + 1)
            kv_s[kind][head] = wide[:, at:at + HEAD].T.astype(jnp.bfloat16)

        @pl.when(me < n - 1)
        def _():
            for kind in range(2):
                shift(kind, head).start()

    owns = []
    for h in range(HEADS):
        at = 3 * HEAD * h
        q = wide[:, at:at + HEAD].astype(jnp.bfloat16)
        k_own = wide[:, at + HEAD:at + 2 * HEAD].astype(jnp.bfloat16).astype(jnp.float32)
        own = jnp.sum(q.astype(jnp.float32) * k_own, axis=-1, keepdims=True) * inv_root
        owns.append(own)

    loads[5].wait()
    pieces = spans([0] + [HEAD * h // 128 * 128 for h in range(2, HEADS)] + [att])
    for h in range(HEADS):
        @pl.when(me > 0)
        def _():
            shift(0, h).wait_recv()
        at = 3 * HEAD * h
        q = wide[:, at:at + HEAD].astype(jnp.bfloat16)
        v_own = wide[:, at + 2 * HEAD:at + 3 * HEAD].astype(jnp.bfloat16).astype(jnp.float32)
        own = owns[h]
        far = jnp.where(me > 0, jnp.dot(q, kv_r[0][h], preferred_element_type=jnp.float32) * inv_root, -jnp.inf)
        top = jnp.maximum(jnp.max(far, axis=-1, keepdims=True), own)
        far_lifted = jnp.exp(far - top)
        own_lifted = jnp.exp(own - top)
        share = 1.0 / (jnp.sum(far_lifted, axis=-1, keepdims=True) + own_lifted)
        far_probs = (far_lifted * share).astype(jnp.bfloat16)
        own_probs = (own_lifted * share).astype(jnp.bfloat16).astype(jnp.float32)
        own_part = own_probs * v_own
        if h >= 2:
            lo, hi = pieces[h - 2]
            back = mixed[:, lo:hi].astype(jnp.bfloat16)
            for a, b in cuts(depth, 512):
                resid[:, a:b] += jnp.dot(back, wo_v[1, lo:hi, a:b], preferred_element_type=jnp.float32)

        @pl.when(me > 0)
        def _():
            shift(1, h).wait_recv()
        mixed[:, HEAD * h:HEAD * (h + 1)] = dot_nt(far_probs, kv_r[1][h]) + own_part

    lo, hi = pieces[-1]
    back = mixed[:, lo:hi].astype(jnp.bfloat16)
    for a, b in cuts(depth, 512):
        out_ref[:, a:b] = (resid[:, a:b] + jnp.dot(
            back, wo_v[1, lo:hi, a:b], preferred_element_type=jnp.float32)).astype(jnp.bfloat16)

    settle_all(ids_all, ids_ss)
    settle_all(emb_s, emb_ss)
    for part in range(len(qkv)):
        settle_all(qkv_s[part], qkv_ss.at[part])
    for part in range(len(mix)):
        settle_all(mix_s[part], mix_ss.at[part])

    @pl.when(me < n - 1)
    def _():
        for kind in range(2):
            for head in range(HEADS):
                shift(kind, head).wait_send()


def solution(mesh):
    n = mesh.shape["seq"]

    def shards(song_ids, table, position_table, w_qkv, w_out):
        tokens, depth = position_table.shape
        vocab, features = table.shape
        layers, _, width = w_qkv.shape
        att = w_out.shape[1]
        cols = tokens // n
        bf16, f32 = jnp.bfloat16, jnp.float32
        hbm = pl.BlockSpec(memory_space=pl.ANY)
        qkv = [pltpu.VMEM((n, cols, b - a), bf16) for a, b in qkv_spans(width)]
        mix = [pltpu.VMEM((n, cols, b - a), bf16) for a, b in mix_spans(att)]
        kv = [pltpu.VMEM((HEADS, HEAD, tokens), bf16)] * 2
        sems = pltpu.SemaphoreType.DMA
        return pl.pallas_call(
            functools.partial(kernel, n),
            out_shape=pltpu.VMEM((tokens, depth), bf16),
            in_specs=[hbm, hbm, hbm, hbm, hbm],
            out_specs=pl.BlockSpec(memory_space=pltpu.VMEM),
            scratch_shapes=[
                pltpu.VMEM((tokens, depth), bf16),
                pltpu.VMEM((layers, width, depth), bf16),
                pltpu.VMEM((layers, att, depth), bf16),
                pltpu.VMEM((features, vocab), bf16),
                pltpu.VMEM((n, 1, tokens), jnp.int32),
                pltpu.VMEM((n, features, tokens), bf16),
                pltpu.VMEM((n, features, tokens), bf16),
                pltpu.VMEM((depth, tokens), f32),
                pltpu.VMEM((tokens, depth), f32),
                pltpu.VMEM((tokens, depth), bf16),
                qkv, list(qkv),
                pltpu.VMEM((depth, width), bf16),
                pltpu.VMEM((tokens, width), f32),
                mix, list(mix),
                pltpu.VMEM((tokens, att), f32),
                kv, list(kv),
                sems((7,)),
                sems, sems((n,)), sems, sems,
                sems((len(qkv),)), sems((len(qkv),)), sems((len(mix),)), sems((len(mix),)),
                sems((2, HEADS)), sems((2, HEADS)),
            ],
            compiler_params=pltpu.CompilerParams(
                collective_id=0, has_side_effects=True, vmem_limit_bytes=56 << 20),
            name="music_rows",
        )(song_ids.reshape(1, tokens), table.T, position_table, jnp.swapaxes(w_qkv, 1, 2), w_out)

    in_specs = (P(("song", "seq")), P(None, "seq"), P("seq", None), P(), P())
    out_specs = P(("song", "seq"), None)
    return jax.shard_map(shards, mesh=mesh, in_specs=in_specs, out_specs=out_specs, check_vma=False)
```

```python
import functools
import math

import jax
import jax.numpy as jnp
from jax import lax
from jax.experimental import pallas as pl
from jax.experimental.pallas import tpu as pltpu
from jax.sharding import PartitionSpec as P

HEADS = 4
HEAD = 150
MESH = pl.DeviceIdType.MESH

epsilon = 1e-05
inv_root = 1.0 / math.sqrt(HEAD)


def cuts(width, step):
    return [(a, min(a + step, width)) for a in range(0, width, step)]


def spans(edges):
    return list(zip(edges[:-1], edges[1:]))


def head_spans(width):
    return spans([0] + [min(-(-3 * HEAD * (h + 1) // 128) * 128, width) for h in range(HEADS)])


def qkv_spans(width):
    heads = head_spans(width)
    return [(0, heads[1][1])] + heads[2:]


def mix_spans(att):
    return spans([0, 2 * HEAD // 128 * 128, 3 * HEAD // 128 * 128, att])


def normalize_into(resid, normed):
    value = resid[...]
    mean = jnp.mean(value, axis=-1, keepdims=True)
    centered = value - mean
    variance = jnp.mean(centered * centered, axis=-1, keepdims=True)
    normed[...] = (centered * lax.rsqrt(variance + epsilon)).astype(jnp.bfloat16)


def dot_nt(a, b):
    dims = (((1,), (1,)), ((), ()))
    return lax.dot_general(a, b, dims, preferred_element_type=jnp.float32)


def scores_of(q, k):
    return dot_nt(q, k) * inv_root


def kernel(n, ids_hbm, table_hbm, pos_hbm, wqkv_hbm, wout_hbm, out_ref,
           pos_v, wq_v, wo_v, table_t, ids_all, emb_s, emb_r, emb_t, resid, normed,
           qkv_s, qkv_r, wt, wide, mix_s, mix_r, mixed, kv_s, kv_r,
           load_sem, ids_ss, ids_rs, emb_ss, emb_rs, qkv_ss, qkv_rs, mix_ss, mix_rs, kv_ss, kv_rs):
    me = lax.axis_index("seq")
    features, vocab = table_t.shape
    tokens, depth = resid.shape
    cols = tokens // n
    width = wide.shape[1]
    att = mixed.shape[1]
    others = list(range(n // 2, n)) + list(range(1, n // 2))
    parity = me & 1

    def send(src, dst, ss, rs, k):
        return pltpu.make_async_remote_copy(
            src_ref=src, dst_ref=dst, send_sem=ss, recv_sem=rs,
            device_id={"seq": me ^ k}, device_id_type=MESH)

    def settle(ref, sem):
        pltpu.make_async_copy(ref, ref, sem).wait()

    def settle_all(ref, sem):
        settle(ref.at[pl.ds(0, n - 1)], sem)

    loads = [pltpu.make_async_copy(table_hbm, table_t, load_sem.at[0]),
             pltpu.make_async_copy(pos_hbm, pos_v, load_sem.at[1])]
    for layer in range(2):
        loads.append(pltpu.make_async_copy(wqkv_hbm.at[layer], wq_v.at[layer], load_sem.at[2 + 2 * layer]))
        loads.append(pltpu.make_async_copy(wout_hbm.at[layer], wo_v.at[layer], load_sem.at[3 + 2 * layer]))
    own_ids = ids_all.at[me]
    ids_load = pltpu.make_async_copy(ids_hbm, own_ids, load_sem.at[6])
    ids_load.start()
    loads[0].start()

    barrier = pltpu.get_barrier_semaphore()
    for k in others:
        pl.semaphore_signal(barrier, inc=1, device_id={"seq": me ^ k}, device_id_type=MESH)
    ids_load.wait()
    pl.semaphore_wait(barrier, n - 1)

    for k in others:
        send(own_ids, own_ids, ids_ss, ids_rs.at[k], k).start()
    loads[0].wait()
    for load in loads[1:]:
        load.start()

    def gather(ids):
        codes = lax.broadcasted_iota(jnp.int32, (vocab, tokens), 0)
        hot = jnp.where(codes == ids, 1.0, 0.0).astype(jnp.bfloat16)
        return jnp.dot(table_t[...], hot, preferred_element_type=jnp.float32).astype(jnp.bfloat16)

    def serve(step, carry):
        group, turn = step // (n // 2), lax.rem(step, n // 2)
        k = 2 * (n // 2 - 1 - turn) + (group ^ parity)
        peer = me ^ k

        @pl.when(k > 0)
        def _():
            settle(ids_all.at[peer], ids_rs.at[k])

        emb_s[peer] = gather(ids_all[peer])

        @pl.when(k > 0)
        def _():
            send(emb_s.at[peer], emb_r.at[me], emb_ss, emb_rs, k).start()
        return carry

    lax.fori_loop(0, n, serve, 0)
    emb_r[me] = emb_s[me]

    def turn_weights():
        loads[4].wait()

        def strip(i, carry):
            at = pl.multiple_of(i * 128, 128)
            for a, b in cuts(width, 128):
                wt[pl.ds(at, 128), a:b] = wq_v[1, a:b, pl.ds(at, 128)].T
            return carry

        lax.fori_loop(0, depth // 128, strip, 0)

    @pl.when(parity == 1)
    def _():
        turn_weights()

    settle_all(emb_r, emb_rs)
    for src in range(n):
        emb_t[src * features:(src + 1) * features, :] = emb_r[src].astype(jnp.float32)
    loads[1].wait()
    for a, b in cuts(depth, 128):
        resid[:, a:b] = emb_t[a:b, :].T + pos_v[:, a:b].astype(jnp.float32)

    normalize_into(resid, normed)
    loads[2].wait()
    qkv = qkv_spans(width)
    for part, (a, b) in enumerate(qkv):
        wide[:, a:b] = dot_nt(normed[...], wq_v[0, a:b, :])
        for dst in range(n):
            qkv_s[part][dst] = wide[dst * cols:(dst + 1) * cols, a:b].astype(jnp.bfloat16)
        for k in others:
            send(qkv_s[part].at[me ^ k], qkv_r[part].at[me], qkv_ss.at[part], qkv_rs.at[part], k).start()
        qkv_r[part][me] = qkv_s[part][me]

    @pl.when(parity == 0)
    def _():
        turn_weights()

    first = lax.broadcasted_iota(jnp.int32, (tokens, tokens), 0)
    second = lax.broadcasted_iota(jnp.int32, (tokens, tokens), 1)
    allowed = (((first - second) & (cols - 1)) == 0) & (second <= first)
    mix = mix_spans(att)
    sent = 0
    for h in range(HEADS):
        if h != 1:
            part = max(h - 1, 0)
            a, b = qkv[part]
            settle_all(qkv_r[part], qkv_rs.at[part])
            for src in range(n):
                wide[src * cols:(src + 1) * cols, a:b] = qkv_r[part][src].astype(jnp.float32)
        at = 3 * HEAD * h
        q = wide[:, at:at + HEAD].astype(jnp.bfloat16)
        k = wide[:, at + HEAD:at + 2 * HEAD].astype(jnp.bfloat16)
        v = wide[:, at + 2 * HEAD:at + 3 * HEAD].astype(jnp.bfloat16)
        scores = jnp.where(allowed, scores_of(q, k), -jnp.inf)
        lifted = jnp.exp(scores - jnp.max(scores, axis=-1, keepdims=True))
        probs = (lifted * (1.0 / jnp.sum(lifted, axis=-1, keepdims=True))).astype(jnp.bfloat16)
        mixed[:, HEAD * h:HEAD * (h + 1)] = jnp.dot(probs, v, preferred_element_type=jnp.float32)
        while sent < len(mix) and mix[sent][1] <= HEAD * (h + 1):
            a, b = mix[sent]
            for dst in range(n):
                mix_s[sent][dst] = mixed[dst * cols:(dst + 1) * cols, a:b].astype(jnp.bfloat16)
            for k in others:
                send(mix_s[sent].at[me ^ k], mix_r[sent].at[me], mix_ss.at[sent], mix_rs.at[sent], k).start()
            mix_r[sent][me] = mix_s[sent][me]
            sent += 1

    def receive_mix(part):
        a, b = mix[part]
        settle_all(mix_r[part], mix_rs.at[part])
        for src in range(n):
            mixed[src * cols:(src + 1) * cols, a:b] = mix_r[part][src].astype(jnp.float32)

    loads[3].wait()
    for part, (lo, hi) in enumerate(mix):
        receive_mix(part)
        back = mixed[:, lo:hi].astype(jnp.bfloat16)
        shift_by, first_sum, second_sum = None, None, None
        for a, b in cuts(depth, 512):
            value = resid[:, a:b] + jnp.dot(back, wo_v[0, lo:hi, a:b], preferred_element_type=jnp.float32)
            resid[:, a:b] = value
            if part < len(mix) - 1:
                continue
            if shift_by is None:
                shift_by = jnp.mean(value[:, :128], axis=-1, keepdims=True)
                first_sum = jnp.zeros((tokens, 128), jnp.float32)
                second_sum = jnp.zeros((tokens, 128), jnp.float32)
            for c in range(0, b - a, 128):
                off = value[:, c:c + 128] - shift_by
                first_sum += off
                second_sum += off * off
    off_mean = jnp.sum(first_sum, axis=-1, keepdims=True) * (1.0 / depth)
    variance = jnp.sum(second_sum, axis=-1, keepdims=True) * (1.0 / depth) - off_mean * off_mean
    scale = lax.rsqrt(variance + epsilon)
    center = shift_by + off_mean
    for a, b in cuts(depth, 512):
        normed[:, a:b] = ((resid[:, a:b] - center) * scale).astype(jnp.bfloat16)

    def shift(kind, head):
        return pltpu.make_async_remote_copy(
            src_ref=kv_s[kind].at[head], dst_ref=kv_r[kind].at[head],
            send_sem=kv_ss.at[kind, head], recv_sem=kv_rs.at[kind, head],
            device_id={"seq": lax.rem(me + 1, n)}, device_id_type=MESH)

    @pl.when(me == 0)
    def _():
        for kind in range(2):
            kv_r[kind][...] = jnp.zeros_like(kv_r[kind])

    for head, (a, b) in enumerate(head_spans(width)):
        wide[:, a:b] = jnp.dot(normed[...], wt[:, a:b], preferred_element_type=jnp.float32)
        for kind in range(2):
            at = 3 * HEAD * head + HEAD * (kind + 1)
            kv_s[kind][head] = wide[:, at:at + HEAD].T.astype(jnp.bfloat16)

        @pl.when(me < n - 1)
        def _():
            for kind in range(2):
                shift(kind, head).start()

    owns = []
    for h in range(HEADS):
        at = 3 * HEAD * h
        q = wide[:, at:at + HEAD].astype(jnp.bfloat16)
        k_own = wide[:, at + HEAD:at + 2 * HEAD].astype(jnp.bfloat16).astype(jnp.float32)
        own = jnp.sum(q.astype(jnp.float32) * k_own, axis=-1, keepdims=True) * inv_root
        owns.append(own)

    loads[5].wait()
    pieces = spans([0] + [HEAD * h // 128 * 128 for h in range(2, HEADS)] + [att])
    for h in range(HEADS):
        @pl.when(me > 0)
        def _():
            shift(0, h).wait_recv()
        at = 3 * HEAD * h
        q = wide[:, at:at + HEAD].astype(jnp.bfloat16)
        v_own = wide[:, at + 2 * HEAD:at + 3 * HEAD].astype(jnp.bfloat16).astype(jnp.float32)
        own = owns[h]
        far = jnp.where(me > 0, jnp.dot(q, kv_r[0][h], preferred_element_type=jnp.float32) * inv_root, -jnp.inf)
        top = jnp.maximum(jnp.max(far, axis=-1, keepdims=True), own)
        far_lifted = jnp.exp(far - top)
        own_lifted = jnp.exp(own - top)
        share = 1.0 / (jnp.sum(far_lifted, axis=-1, keepdims=True) + own_lifted)
        far_probs = (far_lifted * share).astype(jnp.bfloat16)
        own_probs = (own_lifted * share).astype(jnp.bfloat16).astype(jnp.float32)
        own_part = own_probs * v_own
        if h >= 2:
            lo, hi = pieces[h - 2]
            back = mixed[:, lo:hi].astype(jnp.bfloat16)
            for a, b in cuts(depth, 512):
                resid[:, a:b] += jnp.dot(back, wo_v[1, lo:hi, a:b], preferred_element_type=jnp.float32)

        @pl.when(me > 0)
        def _():
            shift(1, h).wait_recv()
        mixed[:, HEAD * h:HEAD * (h + 1)] = dot_nt(far_probs, kv_r[1][h]) + own_part

    lo, hi = pieces[-1]
    back = mixed[:, lo:hi].astype(jnp.bfloat16)
    for a, b in cuts(depth, 512):
        out_ref[:, a:b] = (resid[:, a:b] + jnp.dot(
            back, wo_v[1, lo:hi, a:b], preferred_element_type=jnp.float32)).astype(jnp.bfloat16)

    settle_all(ids_all, ids_ss)
    settle_all(emb_s, emb_ss)
    for part in range(len(qkv)):
        settle_all(qkv_s[part], qkv_ss.at[part])
    for part in range(len(mix)):
        settle_all(mix_s[part], mix_ss.at[part])

    @pl.when(me < n - 1)
    def _():
        for kind in range(2):
            for head in range(HEADS):
                shift(kind, head).wait_send()


def solution(mesh):
    n = mesh.shape["seq"]

    def shards(song_ids, table, position_table, w_qkv, w_out):
        tokens, depth = position_table.shape
        vocab, features = table.shape
        layers, _, width = w_qkv.shape
        att = w_out.shape[1]
        cols = tokens // n
        bf16, f32 = jnp.bfloat16, jnp.float32
        hbm = pl.BlockSpec(memory_space=pl.ANY)
        qkv = [pltpu.VMEM((n, cols, b - a), bf16) for a, b in qkv_spans(width)]
        mix = [pltpu.VMEM((n, cols, b - a), bf16) for a, b in mix_spans(att)]
        kv = [pltpu.VMEM((HEADS, HEAD, tokens), bf16)] * 2
        sems = pltpu.SemaphoreType.DMA
        return pl.pallas_call(
            functools.partial(kernel, n),
            out_shape=pltpu.VMEM((tokens, depth), bf16),
            in_specs=[hbm, hbm, hbm, hbm, hbm],
            out_specs=pl.BlockSpec(memory_space=pltpu.VMEM),
            scratch_shapes=[
                pltpu.VMEM((tokens, depth), bf16),
                pltpu.VMEM((layers, width, depth), bf16),
                pltpu.VMEM((layers, att, depth), bf16),
                pltpu.VMEM((features, vocab), bf16),
                pltpu.VMEM((n, 1, tokens), jnp.int32),
                pltpu.VMEM((n, features, tokens), bf16),
                pltpu.VMEM((n, features, tokens), bf16),
                pltpu.VMEM((depth, tokens), f32),
                pltpu.VMEM((tokens, depth), f32),
                pltpu.VMEM((tokens, depth), bf16),
                qkv, list(qkv),
                pltpu.VMEM((depth, width), bf16),
                pltpu.VMEM((tokens, width), f32),
                mix, list(mix),
                pltpu.VMEM((tokens, att), f32),
                kv, list(kv),
                sems((7,)),
                sems, sems((n,)), sems, sems,
                sems((len(qkv),)), sems((len(qkv),)), sems((len(mix),)), sems((len(mix),)),
                sems((2, HEADS)), sems((2, HEADS)),
            ],
            compiler_params=pltpu.CompilerParams(
                collective_id=0, has_side_effects=True, vmem_limit_bytes=56 << 20),
            name="music_rows",
        )(song_ids.reshape(1, tokens), table.T, position_table, jnp.swapaxes(w_qkv, 1, 2), w_out)

    in_specs = (P(("song", "seq")), P(None, "seq"), P("seq", None), P(), P())
    out_specs = P(("song", "seq"), None)
    return jax.shard_map(shards, mesh=mesh, in_specs=in_specs, out_specs=out_specs, check_vma=False)
```

```python
import functools
import math

import jax
import jax.numpy as jnp
from jax import lax
from jax.experimental import pallas as pl
from jax.experimental.pallas import tpu as pltpu
from jax.sharding import PartitionSpec as P

HEADS = 4
HEAD = 150
MESH = pl.DeviceIdType.MESH

epsilon = 1e-05
inv_root = 1.0 / math.sqrt(HEAD)


def cuts(width, step):
    return [(a, min(a + step, width)) for a in range(0, width, step)]


def spans(edges):
    return list(zip(edges[:-1], edges[1:]))


def head_spans(width):
    return spans([0] + [min(-(-3 * HEAD * (h + 1) // 128) * 128, width) for h in range(HEADS)])


def qkv_spans(width):
    heads = head_spans(width)
    return [(0, heads[1][1])] + heads[2:]


def mix_spans(att):
    return spans([0, 2 * HEAD // 128 * 128, 3 * HEAD // 128 * 128, att])


def normalize_into(resid, normed):
    value = resid[...]
    mean = jnp.mean(value, axis=-1, keepdims=True)
    centered = value - mean
    variance = jnp.mean(centered * centered, axis=-1, keepdims=True)
    normed[...] = (centered * lax.rsqrt(variance + epsilon)).astype(jnp.bfloat16)


def dot_nt(a, b):
    dims = (((1,), (1,)), ((), ()))
    return lax.dot_general(a, b, dims, preferred_element_type=jnp.float32)


def scores_of(q, k):
    return dot_nt(q, k) * inv_root


def kernel(n, ids_hbm, table_hbm, pos_hbm, wqkv_hbm, wout_hbm, out_ref,
           pos_v, wq_v, wo_v, table_t, ids_all, emb_s, emb_r, emb_t, resid, normed,
           qkv_s, qkv_r, wt, wide, mix_s, mix_r, mixed, kv_s, kv_r,
           load_sem, ids_ss, ids_rs, emb_ss, emb_rs, qkv_ss, qkv_rs, mix_ss, mix_rs, kv_ss, kv_rs):
    me = lax.axis_index("seq")
    features, vocab = table_t.shape
    tokens, depth = resid.shape
    cols = tokens // n
    width = wide.shape[1]
    att = mixed.shape[1]
    others = list(range(n // 2, n)) + list(range(1, n // 2))
    parity = me & 1

    def send(src, dst, ss, rs, k):
        return pltpu.make_async_remote_copy(
            src_ref=src, dst_ref=dst, send_sem=ss, recv_sem=rs,
            device_id={"seq": me ^ k}, device_id_type=MESH)

    def settle(ref, sem):
        pltpu.make_async_copy(ref, ref, sem).wait()

    def settle_all(ref, sem):
        settle(ref.at[pl.ds(0, n - 1)], sem)

    loads = [pltpu.make_async_copy(table_hbm, table_t, load_sem.at[0]),
             pltpu.make_async_copy(pos_hbm, pos_v, load_sem.at[1])]
    for layer in range(2):
        loads.append(pltpu.make_async_copy(wqkv_hbm.at[layer], wq_v.at[layer], load_sem.at[2 + 2 * layer]))
        loads.append(pltpu.make_async_copy(wout_hbm.at[layer], wo_v.at[layer], load_sem.at[3 + 2 * layer]))
    own_ids = ids_all.at[me]
    ids_load = pltpu.make_async_copy(ids_hbm, own_ids, load_sem.at[6])
    ids_load.start()
    loads[0].start()

    barrier = pltpu.get_barrier_semaphore()
    for k in others:
        pl.semaphore_signal(barrier, inc=1, device_id={"seq": me ^ k}, device_id_type=MESH)
    ids_load.wait()
    pl.semaphore_wait(barrier, n - 1)

    for k in range(n - 1, 0, -1):
        send(own_ids, own_ids, ids_ss, ids_rs.at[k], k).start()
    loads[0].wait()
    for load in loads[1:]:
        load.start()

    def gather(ids):
        codes = lax.broadcasted_iota(jnp.int32, (vocab, tokens), 0)
        hot = jnp.where(codes == ids, 1.0, 0.0).astype(jnp.bfloat16)
        return jnp.dot(table_t[...], hot, preferred_element_type=jnp.float32).astype(jnp.bfloat16)

    def serve(step, carry):
        group, turn = step // (n // 2), lax.rem(step, n // 2)
        k = 2 * (n // 2 - 1 - turn) + (group ^ parity)
        peer = me ^ k

        @pl.when(k > 0)
        def _():
            settle(ids_all.at[peer], ids_rs.at[k])

        emb_s[peer] = gather(ids_all[peer])

        @pl.when(k > 0)
        def _():
            send(emb_s.at[peer], emb_r.at[me], emb_ss, emb_rs, k).start()
        return carry

    lax.fori_loop(0, n, serve, 0)
    emb_r[me] = emb_s[me]

    def turn_weights():
        loads[4].wait()

        def strip(i, carry):
            at = pl.multiple_of(i * 128, 128)
            for a, b in cuts(width, 128):
                wt[pl.ds(at, 128), a:b] = wq_v[1, a:b, pl.ds(at, 128)].T
            return carry

        lax.fori_loop(0, depth // 128, strip, 0)

    @pl.when(parity == 1)
    def _():
        turn_weights()

    settle_all(emb_r, emb_rs)
    for src in range(n):
        emb_t[src * features:(src + 1) * features, :] = emb_r[src].astype(jnp.float32)
    loads[1].wait()
    for a, b in cuts(depth, 128):
        resid[:, a:b] = emb_t[a:b, :].T + pos_v[:, a:b].astype(jnp.float32)

    normalize_into(resid, normed)
    loads[2].wait()
    qkv = qkv_spans(width)
    for part, (a, b) in enumerate(qkv):
        wide[:, a:b] = dot_nt(normed[...], wq_v[0, a:b, :])
        for dst in range(n):
            qkv_s[part][dst] = wide[dst * cols:(dst + 1) * cols, a:b].astype(jnp.bfloat16)
        for k in others:
            send(qkv_s[part].at[me ^ k], qkv_r[part].at[me], qkv_ss.at[part], qkv_rs.at[part], k).start()
        qkv_r[part][me] = qkv_s[part][me]

    @pl.when(parity == 0)
    def _():
        turn_weights()

    first = lax.broadcasted_iota(jnp.int32, (tokens, tokens), 0)
    second = lax.broadcasted_iota(jnp.int32, (tokens, tokens), 1)
    allowed = (((first - second) & (cols - 1)) == 0) & (second <= first)
    mix = mix_spans(att)
    sent = 0
    for h in range(HEADS):
        if h != 1:
            part = max(h - 1, 0)
            a, b = qkv[part]
            settle_all(qkv_r[part], qkv_rs.at[part])
            for src in range(n):
                wide[src * cols:(src + 1) * cols, a:b] = qkv_r[part][src].astype(jnp.float32)
        at = 3 * HEAD * h
        q = wide[:, at:at + HEAD].astype(jnp.bfloat16)
        k = wide[:, at + HEAD:at + 2 * HEAD].astype(jnp.bfloat16)
        v = wide[:, at + 2 * HEAD:at + 3 * HEAD].astype(jnp.bfloat16)
        scores = jnp.where(allowed, scores_of(q, k), -jnp.inf)
        lifted = jnp.exp(scores - jnp.max(scores, axis=-1, keepdims=True))
        probs = (lifted * (1.0 / jnp.sum(lifted, axis=-1, keepdims=True))).astype(jnp.bfloat16)
        mixed[:, HEAD * h:HEAD * (h + 1)] = jnp.dot(probs, v, preferred_element_type=jnp.float32)
        while sent < len(mix) and mix[sent][1] <= HEAD * (h + 1):
            a, b = mix[sent]
            for dst in range(n):
                mix_s[sent][dst] = mixed[dst * cols:(dst + 1) * cols, a:b].astype(jnp.bfloat16)
            for k in others:
                send(mix_s[sent].at[me ^ k], mix_r[sent].at[me], mix_ss.at[sent], mix_rs.at[sent], k).start()
            mix_r[sent][me] = mix_s[sent][me]
            sent += 1

    def receive_mix(part):
        a, b = mix[part]
        settle_all(mix_r[part], mix_rs.at[part])
        for src in range(n):
            mixed[src * cols:(src + 1) * cols, a:b] = mix_r[part][src].astype(jnp.float32)

    loads[3].wait()
    for part, (lo, hi) in enumerate(mix):
        receive_mix(part)
        back = mixed[:, lo:hi].astype(jnp.bfloat16)
        shift_by, first_sum, second_sum = None, None, None
        for a, b in cuts(depth, 512):
            value = resid[:, a:b] + jnp.dot(back, wo_v[0, lo:hi, a:b], preferred_element_type=jnp.float32)
            resid[:, a:b] = value
            if part < len(mix) - 1:
                continue
            if shift_by is None:
                shift_by = jnp.mean(value[:, :128], axis=-1, keepdims=True)
                first_sum = jnp.zeros((tokens, 128), jnp.float32)
                second_sum = jnp.zeros((tokens, 128), jnp.float32)
            for c in range(0, b - a, 128):
                off = value[:, c:c + 128] - shift_by
                first_sum += off
                second_sum += off * off
    off_mean = jnp.sum(first_sum, axis=-1, keepdims=True) * (1.0 / depth)
    variance = jnp.sum(second_sum, axis=-1, keepdims=True) * (1.0 / depth) - off_mean * off_mean
    scale = lax.rsqrt(variance + epsilon)
    center = shift_by + off_mean
    for a, b in cuts(depth, 512):
        normed[:, a:b] = ((resid[:, a:b] - center) * scale).astype(jnp.bfloat16)

    def shift(kind, head):
        return pltpu.make_async_remote_copy(
            src_ref=kv_s[kind].at[head], dst_ref=kv_r[kind].at[head],
            send_sem=kv_ss.at[kind, head], recv_sem=kv_rs.at[kind, head],
            device_id={"seq": lax.rem(me + 1, n)}, device_id_type=MESH)

    @pl.when(me == 0)
    def _():
        for kind in range(2):
            kv_r[kind][...] = jnp.zeros_like(kv_r[kind])

    for head, (a, b) in enumerate(head_spans(width)):
        wide[:, a:b] = jnp.dot(normed[...], wt[:, a:b], preferred_element_type=jnp.float32)
        for kind in range(2):
            at = 3 * HEAD * head + HEAD * (kind + 1)
            kv_s[kind][head] = wide[:, at:at + HEAD].T.astype(jnp.bfloat16)

        @pl.when(me < n - 1)
        def _():
            for kind in range(2):
                shift(kind, head).start()

    owns = []
    for h in range(HEADS):
        at = 3 * HEAD * h
        q = wide[:, at:at + HEAD].astype(jnp.bfloat16)
        k_own = wide[:, at + HEAD:at + 2 * HEAD].astype(jnp.bfloat16).astype(jnp.float32)
        own = jnp.sum(q.astype(jnp.float32) * k_own, axis=-1, keepdims=True) * inv_root
        owns.append(own)

    loads[5].wait()
    pieces = spans([0] + [HEAD * h // 128 * 128 for h in range(2, HEADS)] + [att])
    for h in range(HEADS):
        @pl.when(me > 0)
        def _():
            shift(0, h).wait_recv()
        at = 3 * HEAD * h
        q = wide[:, at:at + HEAD].astype(jnp.bfloat16)
        v_own = wide[:, at + 2 * HEAD:at + 3 * HEAD].astype(jnp.bfloat16).astype(jnp.float32)
        own = owns[h]
        far = jnp.where(me > 0, jnp.dot(q, kv_r[0][h], preferred_element_type=jnp.float32) * inv_root, -jnp.inf)
        top = jnp.maximum(jnp.max(far, axis=-1, keepdims=True), own)
        far_lifted = jnp.exp(far - top)
        own_lifted = jnp.exp(own - top)
        share = 1.0 / (jnp.sum(far_lifted, axis=-1, keepdims=True) + own_lifted)
        far_probs = (far_lifted * share).astype(jnp.bfloat16)
        own_probs = (own_lifted * share).astype(jnp.bfloat16).astype(jnp.float32)
        own_part = own_probs * v_own
        if h >= 2:
            lo, hi = pieces[h - 2]
            back = mixed[:, lo:hi].astype(jnp.bfloat16)
            for a, b in cuts(depth, 512):
                resid[:, a:b] += jnp.dot(back, wo_v[1, lo:hi, a:b], preferred_element_type=jnp.float32)

        @pl.when(me > 0)
        def _():
            shift(1, h).wait_recv()
        mixed[:, HEAD * h:HEAD * (h + 1)] = dot_nt(far_probs, kv_r[1][h]) + own_part

    lo, hi = pieces[-1]
    back = mixed[:, lo:hi].astype(jnp.bfloat16)
    for a, b in cuts(depth, 512):
        out_ref[:, a:b] = (resid[:, a:b] + jnp.dot(
            back, wo_v[1, lo:hi, a:b], preferred_element_type=jnp.float32)).astype(jnp.bfloat16)

    settle_all(ids_all, ids_ss)
    settle_all(emb_s, emb_ss)
    for part in range(len(qkv)):
        settle_all(qkv_s[part], qkv_ss.at[part])
    for part in range(len(mix)):
        settle_all(mix_s[part], mix_ss.at[part])

    @pl.when(me < n - 1)
    def _():
        for kind in range(2):
            for head in range(HEADS):
                shift(kind, head).wait_send()


def solution(mesh):
    n = mesh.shape["seq"]

    def shards(song_ids, table, position_table, w_qkv, w_out):
        tokens, depth = position_table.shape
        vocab, features = table.shape
        layers, _, width = w_qkv.shape
        att = w_out.shape[1]
        cols = tokens // n
        bf16, f32 = jnp.bfloat16, jnp.float32
        hbm = pl.BlockSpec(memory_space=pl.ANY)
        qkv = [pltpu.VMEM((n, cols, b - a), bf16) for a, b in qkv_spans(width)]
        mix = [pltpu.VMEM((n, cols, b - a), bf16) for a, b in mix_spans(att)]
        kv = [pltpu.VMEM((HEADS, HEAD, tokens), bf16)] * 2
        sems = pltpu.SemaphoreType.DMA
        return pl.pallas_call(
            functools.partial(kernel, n),
            out_shape=pltpu.VMEM((tokens, depth), bf16),
            in_specs=[hbm, hbm, hbm, hbm, hbm],
            out_specs=pl.BlockSpec(memory_space=pltpu.VMEM),
            scratch_shapes=[
                pltpu.VMEM((tokens, depth), bf16),
                pltpu.VMEM((layers, width, depth), bf16),
                pltpu.VMEM((layers, att, depth), bf16),
                pltpu.VMEM((features, vocab), bf16),
                pltpu.VMEM((n, 1, tokens), jnp.int32),
                pltpu.VMEM((n, features, tokens), bf16),
                pltpu.VMEM((n, features, tokens), bf16),
                pltpu.VMEM((depth, tokens), f32),
                pltpu.VMEM((tokens, depth), f32),
                pltpu.VMEM((tokens, depth), bf16),
                qkv, list(qkv),
                pltpu.VMEM((depth, width), bf16),
                pltpu.VMEM((tokens, width), f32),
                mix, list(mix),
                pltpu.VMEM((tokens, att), f32),
                kv, list(kv),
                sems((7,)),
                sems, sems((n,)), sems, sems,
                sems((len(qkv),)), sems((len(qkv),)), sems((len(mix),)), sems((len(mix),)),
                sems((2, HEADS)), sems((2, HEADS)),
            ],
            compiler_params=pltpu.CompilerParams(
                collective_id=0, has_side_effects=True, vmem_limit_bytes=56 << 20),
            name="music_rows",
        )(song_ids.reshape(1, tokens), table.T, position_table, jnp.swapaxes(w_qkv, 1, 2), w_out)

    in_specs = (P(("song", "seq")), P(None, "seq"), P("seq", None), P(), P())
    out_specs = P(("song", "seq"), None)
    return jax.shard_map(shards, mesh=mesh, in_specs=in_specs, out_specs=out_specs, check_vma=False)
```
